512 devices in a mesh: row: 16 (over y, core), col: 32 (over z, x).
Axes of the slice: x: 4, y: 8, z: 8, core: 2. Of those that a mesh axis runs over, the one named last changes fastest.
Arguments:
- snapshots: bfloat16 [64, 1536, 4096], P(None, 'row', 'col'), may hold values from -870 to 870
Outputs:
- q_blocks: float32 [64, 1536, 4096], P(None, 'row', 'col')
- r_factor: float32 [64, 64], replicated
The draws below stay inside these ranges and needn't reach their ends.
All inputs are finite; a program needn't handle non-finite values.
Results may differ from the reference program's by a relative error of at most 0.0003.
Values may be sent and summed in bfloat16 or wider, within the bound.
No kernel may reach another device: no remote copies, remote signals or barrier semaphores. Data moves between devices by JAX's collectives and lax.ppermute only.
A program may use at most 64 MiB of HBM per device.

```python
import jax
import jax.numpy as jnp
from jax import lax

SNAP = 64
HALF = 16
NROW = 1536
NCOL = 4096


def draw_snapshots(key, part):
    keys = jax.random.split(jax.random.fold_in(key, 7), 4)
    position = jnp.arange(NROW, dtype=jnp.float32) / NROW
    row_scale = jnp.exp(jnp.log(3.0) * position + jax.random.uniform(keys[0], (NROW,), jnp.float32, 0.0, jnp.log(4.0)))
    col_scale = jnp.exp(jax.random.uniform(keys[1], (NCOL,), jnp.float32, 0.0, jnp.log(3.0)))
    snap_scale = jnp.exp(jax.random.uniform(keys[2], (SNAP,), jnp.float32, 0.0, jnp.log(4.0)))
    base = jnp.clip(jax.random.normal(keys[3], (SNAP, NROW, NCOL), jnp.float32), -6.0, 6.0)
    field = base * snap_scale[:, None, None] * row_scale[None, :, None] * col_scale[None, None, :]
    return field.astype(jnp.bfloat16)


def setup_inputs(seed: int = 0) -> dict:
    splits = jax.random.split(jax.random.key(seed), 2)
    snapshots = draw_snapshots(jax.random.fold_in(splits[1], 71), 0)
    return dict(snapshots=snapshots)


def gauss_taps():
    sigma = HALF / 3.0
    offsets = jnp.arange(2 * HALF + 1, dtype=jnp.float32) - HALF
    weights = jnp.exp(-offsets * offsets / (2.0 * sigma * sigma))
    return weights / jnp.sum(weights)

def smooth(plane):
    weights = gauss_taps()
    across = jnp.zeros_like(plane)
    for k in range(2 * HALF + 1):
        across = across + weights[k] * jnp.roll(plane, HALF - k, axis=1)
    result = jnp.zeros_like(plane)
    for k in range(2 * HALF + 1):
        result = result + weights[k] * jnp.roll(across, HALF - k, axis=0)
    return result

def reference(snapshots):
    filtered = lax.map(lambda plane: smooth(plane.astype(jnp.float32)), snapshots)
    flat_field = filtered.reshape(SNAP, NROW * NCOL)
    gram = jnp.dot(flat_field, flat_field.T, precision=lax.Precision.HIGHEST) / (NROW * NCOL)
    lower = jnp.linalg.cholesky(gram)
    basis = lax.linalg.triangular_solve(lower, flat_field, left_side=True, lower=True)
    return (basis.reshape(SNAP, NROW, NCOL), lower.T)
```

```python
import jax
import jax.numpy as jnp
from jax import lax
from jax.sharding import PartitionSpec as P

HALF = 16


def padded(array, sides, width):
    for axis, dim in sides:
        devices, length = (lax.axis_size(axis), array.shape[dim])
        up = [(i, (i + 1) % devices) for i in range(devices)]
        down = [(j, i) for i, j in up]
        last = lax.slice_in_dim(array, length - width, length, axis=dim)
        initial = lax.slice_in_dim(array, 0, width, axis=dim)
        before = lax.ppermute(last, axis, up)
        after = lax.ppermute(initial, axis, down)
        array = jnp.concatenate([before, array, after], axis=dim)
    return array


def band_matrix(length):
    sigma = HALF / 3.0
    offsets = jnp.arange(2 * HALF + 1, dtype=jnp.float32) - HALF
    total = jnp.sum(jnp.exp(-offsets * offsets / (2.0 * sigma * sigma)))
    outer = jnp.arange(length + 2 * HALF)[:, None]
    inner = jnp.arange(length)[None, :]
    spread = outer - inner
    shifted = (spread - HALF).astype(jnp.float32)
    inside = (spread >= 0) & (spread <= 2 * HALF)
    return jnp.where(inside, jnp.exp(-shifted * shifted / (2.0 * sigma * sigma)) / total, 0.0)


def filter_columns(field):
    width = field.shape[2] - 2 * HALF
    return jnp.einsum("src,cd->srd", field, band_matrix(width), precision=lax.Precision.HIGH)


def filter_rows(field):
    height = field.shape[1] - 2 * HALF
    return jnp.einsum("src,rq->sqc", field, band_matrix(height), precision=lax.Precision.HIGH)


def pack(gram):
    half = gram.shape[0] // 2
    first, second = gram[:half, :half], gram[half:, half:]
    row = lax.broadcasted_iota(jnp.int32, (half, half), 0)
    col = lax.broadcasted_iota(jnp.int32, (half, half), 1)
    mixed = jnp.where(row >= col, first, second)
    diagonal = jnp.sum(jnp.where(row == col, second, 0.0), axis=0)
    diagonal = jnp.pad(diagonal, (0, half))[None]
    top = jnp.concatenate([gram[half:, :half], mixed], axis=1)
    return jnp.concatenate([top, diagonal, jnp.zeros_like(diagonal)], axis=0)


def unpack(packed):
    half = packed.shape[1] // 2
    cross, mixed, diagonal = packed[:half, :half], packed[:half, half:], packed[half, :half]
    row = lax.broadcasted_iota(jnp.int32, (half, half), 0)
    col = lax.broadcasted_iota(jnp.int32, (half, half), 1)
    first = jnp.where(row >= col, mixed, mixed.T)
    second = jnp.where(row < col, mixed, mixed.T)
    second = jnp.where(row == col, diagonal[None], second)
    return jnp.concatenate(
        [jnp.concatenate([first, cross.T], axis=1), jnp.concatenate([cross, second], axis=1)], axis=0
    )


def summed(array, axis):
    copies = jnp.broadcast_to(array[None], (lax.axis_size(axis),) + array.shape)
    return lax.all_to_all(copies, axis, 0, 0).sum(0)


def local(snapshots):
    count, height, width = snapshots.shape
    extended = padded(snapshots, (("row", 1), ("col", 2)), HALF)
    filtered = filter_rows(filter_columns(extended.astype(jnp.float32)))
    points = height * width * lax.axis_size("row") * lax.axis_size("col")
    flat_field = filtered.reshape(count, height * width)
    local_gram = jnp.dot(flat_field, flat_field.T, precision=lax.Precision.HIGH) / points
    total = pack(local_gram).reshape(-1)
    total = summed(summed(total, "row"), "col")
    gram = unpack(total.reshape(count // 2 + 2, count))
    upper = jnp.linalg.cholesky(gram, symmetrize_input=False).T
    inverse = lax.linalg.triangular_solve(upper.T, jnp.eye(count, dtype=jnp.float32), left_side=True, lower=True)
    basis = jnp.dot(inverse, flat_field, precision=lax.Precision.HIGH)
    return (basis.reshape(count, height, width), upper)


def solution(mesh):
    return jax.shard_map(
        local,
        mesh=mesh,
        in_specs=(P(None, "row", "col"),),
        out_specs=(P(None, "row", "col"), P()),
        check_vma=False,
    )
```

```python
import functools
import jax
import jax.numpy as jnp
import numpy as np
from jax import lax
from jax.experimental import pallas as pl
from jax.experimental.pallas import tpu as pltpu
from jax.sharding import PartitionSpec as P

HALF = 16
TAPS = 2 * HALF + 1
BF16, F32 = jnp.bfloat16, jnp.float32
STEP = 48


def band(length):
    sigma = HALF / 3.0
    offsets = np.arange(TAPS) - HALF
    weights = np.exp(-offsets * offsets / (2.0 * sigma * sigma))
    weights = weights / weights.sum()
    result = np.zeros((length + 2 * HALF, length), np.float64)
    for inner in range(length):
        result[inner : inner + TAPS, inner] = weights
    return result


def two(matrix):
    high = np.asarray(matrix, np.float32).astype(BF16)
    low = (matrix - high.astype(np.float64)).astype(np.float32).astype(BF16)
    return high, low


def row_weights(height):
    return np.concatenate([part.T for part in two(band(height))], axis=0)


def column_weights(width):
    matrix = band(width)
    left, own, right = matrix[:HALF], matrix[HALF : HALF + width], matrix[HALF + width :]
    result = []
    for h in range(2):
        for q in range(4):
            halo = np.zeros((width, width))
            first, second = (left, right) if h == 0 else (right, left)
            halo[32 * q : 32 * q + HALF] = first
            halo[32 * q + HALF : 32 * q + 2 * HALF] = second
            result.append(np.concatenate(two(np.concatenate([own, halo], axis=0)), axis=1))
    return np.stack(result)


def strip_selector(width):
    result = np.zeros((8, width, 2 * width), np.float32)
    for h in range(2):
        for q in range(4):
            for c in range(HALF):
                result[4 * h + q, width - HALF + c, 32 * q + HALF * h + c] = 1
                result[4 * h + q, c, width + 32 * q + HALF * (1 - h) + c] = 1
    return result.reshape(8 * width, 2 * width).astype(BF16)


def dot(a, b):
    return jnp.dot(a, b, preferred_element_type=F32)


def split(value):
    high = value.astype(BF16)
    return high, (value - high.astype(F32)).astype(BF16)


def strips_kernel(top, own, bottom, select, last, first):
    width = own.shape[3]
    for g in range(8):
        parts = [jnp.concatenate([top[g, k], own[g, k], bottom[g, k]], axis=0) for k in range(8)]
        both = dot(jnp.concatenate(parts, axis=1), select[...]).astype(BF16)
        last[g] = both[:, :width]
        first[g] = both[:, width:]


def rows_kernel(top, own, bottom, weights, high, low):
    height, width = own.shape[2:]
    for g in range(8):
        for k in range(0, 8, 2):
            parts = [jnp.concatenate([top[g, i], own[g, i], bottom[g, i]], axis=0) for i in (k, k + 1)]
            both = dot(weights[...], jnp.concatenate(parts, axis=1))
            upper, lower = split(both[:height] + both[height:])
            high[g, k], high[g, k + 1] = upper[:, :width], upper[:, width:]
            low[g, k], low[g, k + 1] = lower[:, :width], lower[:, width:]


def columns_kernel(points, high, low, left, right, weights, across, field, packed, halo_high, halo_low, flat):
    height, width = high.shape[2:]
    lane = lax.broadcasted_iota(jnp.int32, left.shape[1:], 1)
    even = (lane // HALF) % 2 == 0
    for g in range(8):
        a, b = left[g].astype(F32), right[g].astype(F32)
        both = jnp.concatenate([jnp.where(even, a, b), jnp.where(even, b, a)], axis=1).astype(BF16)
        both = dot(weights[...], both)
        upper, lower = split(both[:height] + both[height:])
        halo_high[g], halo_low[g] = upper, lower
    for k in range(8):
        lanes = slice(width * (k // 4), width * (k // 4 + 1))
        for g in range(8):
            upper = jnp.concatenate([high[g, k], halo_high[g, :, lanes]], axis=1)
            lower = jnp.concatenate([low[g, k], halo_low[g, :, lanes]], axis=1)
            both = dot(upper, across[k])
            value = both[:, :width] + both[:, width:] + dot(lower, across[k, :, :width])
            flat[pl.ds((8 * g + k) * height, height), :] = value
    count = 64
    for r in range(height):
        upper, lower = split(flat[pl.ds(r, count, stride=height), :])
        field[:count, r * width : (r + 1) * width] = upper
        field[count:, r * width : (r + 1) * width] = lower
    total = jnp.zeros((2 * count, 2 * count), F32)
    size = 2048
    for start in range(0, height * width, size):
        part = field[:, start : start + size]
        total = total + lax.dot_general(part, part, (((1,), (1,)), ((), ())), preferred_element_type=F32)
    gram = total[:count, :count] + total[count:, count:] + (total[:count, count:] + total[count:, :count])
    packed[...] = gram / points


def factor(gram, size=8):
    count = gram.shape[0]
    row = lax.broadcasted_iota(jnp.int32, gram.shape, 0)
    col = lax.broadcasted_iota(jnp.int32, gram.shape, 1)
    a = jnp.concatenate([gram, jnp.where(row == col, 1.0, 0.0).astype(F32)], axis=1)
    rows = []
    for k in range(0, count, size):
        columns = [jnp.broadcast_to(a[:, k + i : k + i + 1], a.shape) for i in range(size)]
        lower, scale = {}, []
        for j in range(size):
            pivot = columns[j][k + j : k + j + 1]
            for m in range(j):
                pivot = pivot - lower[j, m] * lower[j, m]
            scale.append(lax.rsqrt(pivot))
            for i in range(j + 1, size):
                entry = columns[j][k + i : k + i + 1]
                for m in range(j):
                    entry = entry - lower[i, m] * lower[j, m]
                lower[i, j] = entry * scale[j]

        def solve(values):
            done = []
            for i in range(size):
                value = values[i]
                for m in range(i):
                    value = value - lower[i, m] * done[m]
                done.append(value * scale[i])
            return done

        new = solve([a[k + i : k + i + 1] for i in range(size)])
        rows += new
        if k + size < count:
            multipliers = solve(columns)
            for m in range(size):
                a = a - multipliers[m] * new[m]
    return rows


def basis_kernel(gram, field, basis, upper, work, inverse):
    count = gram.shape[0]

    @pl.when(pl.program_id(0) == 0)
    def _():
        for k, value in enumerate(factor(gram[...])):
            work[k : k + 1, :] = value
        row = lax.broadcasted_iota(jnp.int32, (count, count), 0)
        col = lax.broadcasted_iota(jnp.int32, (count, count), 1)
        both = work[...]
        upper[...] = jnp.where(row <= col, both[:, :count], 0.0)
        high, low = split(jnp.where(row >= col, both[:, count:], 0.0))
        top = jnp.concatenate([high, high], axis=1)
        bottom = jnp.concatenate([low, jnp.zeros_like(low)], axis=1)
        inverse[...] = jnp.concatenate([top, bottom], axis=0)

    width = basis.shape[2]
    both = dot(inverse[...], field[...])
    value = both[:count] + both[count:]
    for r in range(basis.shape[1]):
        basis[:, r, :] = value[:, r * width : (r + 1) * width]


def whole(n):
    return [pl.BlockSpec(memory_space=pltpu.VMEM)] * n


def shape(*dims, dtype=BF16):
    return jax.ShapeDtypeStruct(dims, dtype)


def strips(top, own, bottom):
    height, width = own.shape[1] + 2 * HALF, own.shape[2]
    args = [v.reshape(8, 8, *v.shape[1:]) for v in (top, own, bottom)]
    return pl.pallas_call(
        strips_kernel,
        out_shape=[shape(8, height, width)] * 2,
        in_specs=whole(4),
        out_specs=whole(2),
        compiler_params=pltpu.CompilerParams(vmem_limit_bytes=16 << 20),
    )(*args, jnp.asarray(strip_selector(width)))


def filter_rows(top, own, bottom):
    height, width = own.shape[1:]
    args = [v.reshape(8, 8, *v.shape[1:]) for v in (top, own, bottom)]
    return pl.pallas_call(
        rows_kernel,
        out_shape=[shape(8, 8, height, width)] * 2,
        in_specs=whole(4),
        out_specs=whole(2),
        compiler_params=pltpu.CompilerParams(vmem_limit_bytes=16 << 20),
        cost_estimate=pl.CostEstimate(
            flops=4 * own.size * (height + 2 * HALF), bytes_accessed=6 * own.size, transcendentals=0
        ),
    )(*args, jnp.asarray(row_weights(height)))


def filter_columns(high, low, left, right, points):
    height, width = high.shape[2:]
    return pl.pallas_call(
        functools.partial(columns_kernel, points),
        out_shape=[shape(128, height * width), shape(64, 64, dtype=F32)],
        in_specs=whole(6),
        out_specs=whole(2),
        compiler_params=pltpu.CompilerParams(vmem_limit_bytes=24 << 20),
        scratch_shapes=[pltpu.VMEM((8, height, 2 * width), BF16)] * 2 + [pltpu.VMEM((64 * height, width), F32)],
    )(high, low, left, right, jnp.asarray(row_weights(height)), jnp.asarray(column_weights(width)))


def orthonormal(gram, field, height, width):
    count = gram.shape[0]
    return pl.pallas_call(
        basis_kernel,
        grid=(height // STEP,),
        compiler_params=pltpu.CompilerParams(vmem_limit_bytes=24 << 20),
        out_shape=[shape(count, height, width, dtype=F32), shape(count, count, dtype=F32)],
        in_specs=[pl.BlockSpec((count, count), lambda i: (0, 0)), pl.BlockSpec((2 * count, STEP * width), lambda i: (0, i))],
        out_specs=[pl.BlockSpec((count, STEP, width), lambda i: (0, i, 0)), pl.BlockSpec((count, count), lambda i: (0, 0))],
        scratch_shapes=[pltpu.VMEM((count, 2 * count), F32), pltpu.VMEM((2 * count, 2 * count), BF16)],
    )(gram, field)


def pack(gram):
    half = gram.shape[0] // 2
    first, second = gram[:half, :half], gram[half:, half:]
    row = lax.broadcasted_iota(jnp.int32, (half, half), 0)
    col = lax.broadcasted_iota(jnp.int32, (half, half), 1)
    mixed = jnp.where(row >= col, first, second)
    diagonal = jnp.sum(jnp.where(row == col, second, 0.0), axis=0)
    diagonal = jnp.pad(diagonal, (0, half))[None]
    top = jnp.concatenate([gram[half:, :half], mixed], axis=1)
    return jnp.concatenate([top, diagonal, jnp.zeros_like(diagonal)], axis=0)


def unpack(packed):
    half = packed.shape[1] // 2
    cross, mixed, diagonal = packed[:half, :half], packed[:half, half:], packed[half, :half]
    row = lax.broadcasted_iota(jnp.int32, (half, half), 0)
    col = lax.broadcasted_iota(jnp.int32, (half, half), 1)
    first = jnp.where(row >= col, mixed, mixed.T)
    second = jnp.where(row < col, mixed, mixed.T)
    second = jnp.where(row == col, diagonal[None], second)
    return jnp.concatenate(
        [jnp.concatenate([first, cross.T], axis=1), jnp.concatenate([cross, second], axis=1)], axis=0
    )


def summed(array, axis):
    copies = jnp.broadcast_to(array[None], (lax.axis_size(axis),) + array.shape)
    return lax.all_to_all(copies, axis, 0, 0).sum(0)


def swap(upward, downward, axis):
    devices = lax.axis_size(axis)
    up = [(i, (i + 1) % devices) for i in range(devices)]
    down = [(j, i) for i, j in up]
    return lax.ppermute(upward, axis, up), lax.ppermute(downward, axis, down)


def local(snapshots):
    count, height, width = snapshots.shape
    points = height * width * lax.axis_size("row") * lax.axis_size("col")
    top, bottom = swap(snapshots[:, height - HALF :], snapshots[:, :HALF], "row")
    left, right = swap(*strips(top, snapshots, bottom), "col")
    high, low = filter_rows(top, snapshots, bottom)
    field, gram = filter_columns(high, low, left, right, points)
    total = pack(gram).reshape(-1)
    total = summed(summed(total, "row"), "col")
    gram = unpack(total.reshape(count // 2 + 2, count))
    return tuple(orthonormal(gram, field, height, width))


def solution(mesh):
    return jax.shard_map(
        local,
        mesh=mesh,
        in_specs=(P(None, "row", "col"),),
        out_specs=(P(None, "row", "col"), P()),
        check_vma=False,
    )
```

```python
import functools
import jax
import jax.numpy as jnp
import numpy as np
from jax import lax
from jax.experimental import pallas as pl
from jax.experimental.pallas import tpu as pltpu
from jax.sharding import PartitionSpec as P

HALF = 16
TAPS = 2 * HALF + 1
BF16, F32 = jnp.bfloat16, jnp.float32
STEP = 48


def band(length):
    sigma = HALF / 3.0
    offsets = np.arange(TAPS) - HALF
    weights = np.exp(-offsets * offsets / (2.0 * sigma * sigma))
    weights = weights / weights.sum()
    result = np.zeros((length + 2 * HALF, length), np.float64)
    for inner in range(length):
        result[inner : inner + TAPS, inner] = weights
    return result


def two(matrix):
    high = np.asarray(matrix, np.float32).astype(BF16)
    low = (matrix - high.astype(np.float64)).astype(np.float32).astype(BF16)
    return high, low


def row_weights(height):
    return np.concatenate([part.T for part in two(band(height))], axis=0)


def column_weights(width):
    matrix = band(width)
    left, own, right = matrix[:HALF], matrix[HALF : HALF + width], matrix[HALF + width :]
    result = []
    for h in range(2):
        for q in range(4):
            halo = np.zeros((width, width))
            first, second = (left, right) if h == 0 else (right, left)
            halo[32 * q : 32 * q + HALF] = first
            halo[32 * q + HALF : 32 * q + 2 * HALF] = second
            result.append(np.concatenate(two(np.concatenate([own, halo], axis=0)), axis=1))
    return np.stack(result)


def dot(a, b):
    return jnp.dot(a, b, preferred_element_type=F32)


def split(value):
    high = value.astype(BF16)
    return high, (value - high.astype(F32)).astype(BF16)


def selector(width):
    row = lax.broadcasted_iota(jnp.int32, (width, width), 0)
    shift = lax.broadcasted_iota(jnp.int32, (width, width), 1) - row
    blocks = []
    for k in range(8):
        h, q = k // 4, k % 4
        last = (shift == 32 * q + HALF * h + HALF - width) & (row >= width - HALF)
        first = (shift == 32 * q + HALF * (1 - h)) & (row < HALF)
        both = [jnp.where(mask, 1.0, 0.0).astype(BF16) for mask in (last, first)]
        blocks.append(jnp.concatenate(both, axis=1))
    return jnp.concatenate(blocks, axis=0)


def edges_kernel(own, last_columns, first_columns, last_rows, first_rows):
    height, width = own.shape[2:]
    parts = [jnp.concatenate([own[g, k] for k in range(8)], axis=1) for g in range(8)]
    both = dot(jnp.concatenate(parts, axis=0), selector(width)).astype(BF16)
    for g in range(8):
        last_columns[g] = both[g * height : (g + 1) * height, :width]
        first_columns[g] = both[g * height : (g + 1) * height, width:]
    last_rows[...] = own[:, :, height - HALF :, :]
    first_rows[...] = own[:, :, :HALF, :]


def rows_kernel(top, own, bottom, weights, high, low):
    height, width = own.shape[2:]
    for g in range(8):
        for k in range(0, 8, 2):
            parts = [jnp.concatenate([top[g, i], own[g, i], bottom[g, i]], axis=0) for i in (k, k + 1)]
            both = dot(weights[...], jnp.concatenate(parts, axis=1))
            upper, lower = split(both[:height] + both[height:])
            high[g, k], high[g, k + 1] = upper[:, :width], upper[:, width:]
            low[g, k], low[g, k + 1] = lower[:, :width], lower[:, width:]


def columns_kernel(points, high, low, left, right, top, bottom, weights, across, field, packed, halo_high, halo_low, flat):
    height, width = high.shape[2:]
    lane = lax.broadcasted_iota(jnp.int32, (height + 2 * HALF, width), 1)
    even = (lane // HALF) % 2 == 0
    for g in range(8):
        a, b = [
            jnp.concatenate([top[i], side[g], bottom[i]], axis=0).astype(F32)
            for side, i in ((left, g), (right, 8 + g))
        ]
        both = jnp.concatenate([jnp.where(even, a, b), jnp.where(even, b, a)], axis=1).astype(BF16)
        both = dot(weights[...], both)
        upper, lower = split(both[:height] + both[height:])
        halo_high[g], halo_low[g] = upper, lower
    for k in range(8):
        lanes = slice(width * (k // 4), width * (k // 4 + 1))
        for g in range(8):
            upper = jnp.concatenate([high[g, k], halo_high[g, :, lanes]], axis=1)
            lower = jnp.concatenate([low[g, k], halo_low[g, :, lanes]], axis=1)
            both = dot(upper, across[k])
            value = both[:, :width] + both[:, width:] + dot(lower, across[k, :, :width])
            flat[pl.ds((8 * g + k) * (height + 8), height), :] = value
    count = 64
    for r in range(height):
        upper, lower = split(flat[pl.ds(r, count, stride=height + 8), :])
        field[:count, r * width : (r + 1) * width] = upper
        field[count:, r * width : (r + 1) * width] = lower
    total = jnp.zeros((2 * count, 2 * count), F32)
    size = 2048
    for start in range(0, height * width, size):
        part = field[:, start : start + size]
        total = total + lax.dot_general(part, part, (((1,), (1,)), ((), ())), preferred_element_type=F32)
    gram = total[:count, :count] + total[count:, count:] + (total[:count, count:] + total[count:, :count])
    packed[...] = gram / points


def factor(gram, size=8):
    count = gram.shape[0]
    row = lax.broadcasted_iota(jnp.int32, gram.shape, 0)
    col = lax.broadcasted_iota(jnp.int32, gram.shape, 1)
    a = jnp.concatenate([gram, jnp.where(row == col, 1.0, 0.0).astype(F32)], axis=1)
    rows = []
    for k in range(0, count, size):
        columns = [jnp.broadcast_to(a[:, k + i : k + i + 1], a.shape) for i in range(size)]
        lower, scale = {}, []
        for j in range(size):
            pivot = columns[j][k + j : k + j + 1]
            for m in range(j):
                pivot = pivot - lower[j, m] * lower[j, m]
            scale.append(lax.rsqrt(pivot))
            for i in range(j + 1, size):
                entry = columns[j][k + i : k + i + 1]
                for m in range(j):
                    entry = entry - lower[i, m] * lower[j, m]
                lower[i, j] = entry * scale[j]

        def solve(values):
            done = []
            for i in range(size):
                value = values[i]
                for m in range(i):
                    value = value - lower[i, m] * done[m]
                done.append(value * scale[i])
            return done

        new = solve([a[k + i : k + i + 1] for i in range(size)])
        rows += new
        if k + size < count:
            multipliers = solve(columns)
            for m in range(size):
                a = a - multipliers[m] * new[m]
    return rows


def basis_kernel(gram, field, basis, upper, work, inverse):
    count = gram.shape[0]

    @pl.when(pl.program_id(0) == 0)
    def _():
        for k, value in enumerate(factor(gram[...])):
            work[k : k + 1, :] = value
        row = lax.broadcasted_iota(jnp.int32, (count, count), 0)
        col = lax.broadcasted_iota(jnp.int32, (count, count), 1)
        both = work[...]
        upper[...] = jnp.where(row <= col, both[:, :count], 0.0)
        high, low = split(jnp.where(row >= col, both[:, count:], 0.0))
        top = jnp.concatenate([high, high], axis=1)
        bottom = jnp.concatenate([low, jnp.zeros_like(low)], axis=1)
        inverse[...] = jnp.concatenate([top, bottom], axis=0)

    width = basis.shape[2]
    both = dot(inverse[...], field[...])
    value = both[:count] + both[count:]
    for r in range(basis.shape[1]):
        basis[:, r, :] = value[:, r * width : (r + 1) * width]


def whole(n):
    return [pl.BlockSpec(memory_space=pltpu.VMEM)] * n


def shape(*dims, dtype=BF16):
    return jax.ShapeDtypeStruct(dims, dtype)


def edges(own):
    height, width = own.shape[2:]
    return pl.pallas_call(
        edges_kernel,
        out_shape=[shape(8, height, width)] * 2 + [shape(8, 8, HALF, width)] * 2,
        in_specs=whole(1),
        out_specs=whole(4),
        compiler_params=pltpu.CompilerParams(vmem_limit_bytes=16 << 20),
        cost_estimate=pl.CostEstimate(
            flops=4 * width * own.size, bytes_accessed=3 * own.size, transcendentals=0
        ),
    )(own)


def filter_rows(top, own, bottom):
    height, width = own.shape[2:]
    return pl.pallas_call(
        rows_kernel,
        out_shape=[shape(8, 8, height, width)] * 2,
        in_specs=whole(4),
        out_specs=whole(2),
        compiler_params=pltpu.CompilerParams(vmem_limit_bytes=16 << 20),
        cost_estimate=pl.CostEstimate(
            flops=4 * own.size * (height + 2 * HALF), bytes_accessed=6 * own.size, transcendentals=0
        ),
    )(top, own, bottom, jnp.asarray(row_weights(height)))


def filter_columns(high, low, sides, points):
    height, width = high.shape[2:]
    return pl.pallas_call(
        functools.partial(columns_kernel, points),
        out_shape=[shape(128, height * width), shape(64, 64, dtype=F32)],
        in_specs=whole(8),
        out_specs=whole(2),
        compiler_params=pltpu.CompilerParams(vmem_limit_bytes=24 << 20),
        scratch_shapes=[pltpu.VMEM((8, height, 2 * width), BF16)] * 2 + [pltpu.VMEM((64 * (height + 8), width), F32)],
    )(high, low, *sides, jnp.asarray(row_weights(height)), jnp.asarray(column_weights(width)))


def orthonormal(gram, field, height, width):
    count = gram.shape[0]
    return pl.pallas_call(
        basis_kernel,
        grid=(height // STEP,),
        compiler_params=pltpu.CompilerParams(vmem_limit_bytes=24 << 20),
        out_shape=[shape(count, height, width, dtype=F32), shape(count, count, dtype=F32)],
        in_specs=[pl.BlockSpec((count, count), lambda i: (0, 0)), pl.BlockSpec((2 * count, STEP * width), lambda i: (0, i))],
        out_specs=[pl.BlockSpec((count, STEP, width), lambda i: (0, i, 0)), pl.BlockSpec((count, count), lambda i: (0, 0))],
        scratch_shapes=[pltpu.VMEM((count, 2 * count), F32), pltpu.VMEM((2 * count, 2 * count), BF16)],
    )(gram, field)


def pack(gram):
    half = gram.shape[0] // 2
    first, second = gram[:half, :half], gram[half:, half:]
    row = lax.broadcasted_iota(jnp.int32, (half, half), 0)
    col = lax.broadcasted_iota(jnp.int32, (half, half), 1)
    mixed = jnp.where(row >= col, first, second)
    diagonal = jnp.sum(jnp.where(row == col, second, 0.0), axis=0)
    diagonal = jnp.pad(diagonal, (0, half))[None]
    top = jnp.concatenate([gram[half:, :half], mixed], axis=1)
    return jnp.concatenate([top, diagonal, jnp.zeros_like(diagonal)], axis=0)


def unpack(packed):
    half = packed.shape[1] // 2
    cross, mixed, diagonal = packed[:half, :half], packed[:half, half:], packed[half, :half]
    row = lax.broadcasted_iota(jnp.int32, (half, half), 0)
    col = lax.broadcasted_iota(jnp.int32, (half, half), 1)
    first = jnp.where(row >= col, mixed, mixed.T)
    second = jnp.where(row < col, mixed, mixed.T)
    second = jnp.where(row == col, diagonal[None], second)
    return jnp.concatenate(
        [jnp.concatenate([first, cross.T], axis=1), jnp.concatenate([cross, second], axis=1)], axis=0
    )


def summed(array, axis):
    copies = jnp.broadcast_to(array[None], (lax.axis_size(axis),) + array.shape)
    return lax.all_to_all(copies, axis, 0, 0).sum(0)


def swap(upward, downward, axis):
    devices = lax.axis_size(axis)
    up = [(i, (i + 1) % devices) for i in range(devices)]
    down = [(j, i) for i, j in up]
    return lax.ppermute(upward, axis, up), lax.ppermute(downward, axis, down)


def local(snapshots):
    count, height, width = snapshots.shape
    points = height * width * lax.axis_size("row") * lax.axis_size("col")
    own = snapshots.reshape(8, 8, height, width)
    last_columns, first_columns, last_rows, first_rows = edges(own)
    sides = swap(last_columns, first_columns, "col")
    top, bottom = swap(last_rows, first_rows, "row")
    last_rows, first_rows = [
        jnp.concatenate([side[:, rows] for side in sides], axis=0) for rows in (slice(height - HALF, None), slice(HALF))
    ]
    corners = swap(last_rows, first_rows, "row")
    high, low = filter_rows(top, own, bottom)
    field, gram = filter_columns(high, low, (*sides, *corners), points)
    total = pack(gram).reshape(-1)
    total = summed(summed(total, "row"), "col")
    gram = unpack(total.reshape(count // 2 + 2, count))
    return tuple(orthonormal(gram, field, height, width))


def solution(mesh):
    return jax.shard_map(
        local,
        mesh=mesh,
        in_specs=(P(None, "row", "col"),),
        out_specs=(P(None, "row", "col"), P()),
        check_vma=False,
    )
```

```python
import functools
import jax
import jax.numpy as jnp
import numpy as np
from jax import lax
from jax.experimental import pallas as pl
from jax.experimental.pallas import tpu as pltpu
from jax.sharding import PartitionSpec as P


HALF = 16
TAPS = 2 * HALF + 1
BF16, F32 = jnp.bfloat16, jnp.float32
STEP = 48
PAD = 8


def band(length):
    sigma = HALF / 3.0
    offsets = np.arange(TAPS) - HALF
    weights = np.exp(-offsets * offsets / (2.0 * sigma * sigma))
    weights = weights / weights.sum()
    result = np.zeros((length + 2 * HALF, length), np.float64)
    for inner in range(length):
        result[inner : inner + TAPS, inner] = weights
    return result


def two(matrix):
    high = np.asarray(matrix, np.float32).astype(BF16)
    low = (matrix - high.astype(np.float64)).astype(np.float32).astype(BF16)
    return high, low


def row_weights(row, col):
    sigma = HALF / 3.0
    offsets = np.arange(TAPS) - HALF
    total = float(np.exp(-offsets * offsets / (2.0 * sigma * sigma)).sum())
    spread = col - row
    shifted = (spread - HALF).astype(F32)
    value = jnp.exp(shifted * shifted * (-0.5 / (sigma * sigma))) * (1.0 / total)
    value = jnp.where((spread >= 0) & (spread <= 2 * HALF), value, 0.0)
    return jnp.concatenate(split(value), axis=0)


def indices(rows, cols):
    return [lax.broadcasted_iota(jnp.int32, (rows, cols), i) for i in range(2)]


def edge_column_weights(width):
    matrix = band(width)
    edge = np.r_[width - HALF : width, :HALF]
    left, right = matrix[:HALF, edge], matrix[HALF + width :, edge]
    result = []
    for pair in ((left, right), (right, left)):
        block = np.concatenate(pair, axis=0)
        result.append(np.concatenate(two(np.kron(np.eye(4), block)), axis=1))
    return np.stack(result)


def column_weights(width):
    matrix = band(width)
    left, own, right = matrix[:HALF], matrix[HALF : HALF + width], matrix[HALF + width :]
    result = []
    for h in range(2):
        for q in range(4):
            halo = np.zeros((width, width))
            first, second = (left, right) if h == 0 else (right, left)
            halo[32 * q : 32 * q + HALF] = first
            halo[32 * q + HALF : 32 * q + 2 * HALF] = second
            result.append(np.concatenate(two(np.concatenate([own, halo], axis=0)), axis=1))
    return np.stack(result)


def dot(a, b):
    return jnp.dot(a, b, preferred_element_type=F32)


def split(value):
    high = value.astype(BF16)
    return high, (value - high.astype(F32)).astype(BF16)


def selector(width):
    row = lax.broadcasted_iota(jnp.int32, (width, width), 0)
    shift = lax.broadcasted_iota(jnp.int32, (width, width), 1) - row
    blocks = []
    for k in range(8):
        h, q = k // 4, k % 4
        last = (shift == 32 * q + HALF * h + HALF - width) & (row >= width - HALF)
        first = (shift == 32 * q + HALF * (1 - h)) & (row < HALF)
        both = [jnp.where(mask, 1.0, 0.0).astype(BF16) for mask in (last, first)]
        blocks.append(jnp.concatenate(both, axis=1))
    return jnp.concatenate(blocks, axis=0)


def edges_kernel(own, last_columns, first_columns, last_rows, first_rows):
    height, width = own.shape[2:]
    parts = [jnp.concatenate([own[g, k] for k in range(8)], axis=1) for g in range(8)]
    both = dot(jnp.concatenate(parts, axis=0), selector(width)).astype(BF16)
    for g in range(8):
        last_columns[g] = both[g * height : (g + 1) * height, :width]
        first_columns[g] = both[g * height : (g + 1) * height, width:]
    last_rows[...] = own[:, :, height - HALF :, :]
    first_rows[...] = own[:, :, :HALF, :]


def rows_kernel(top, own, bottom, high, low):
    height, width = own.shape[2:]
    weights = row_weights(*indices(height, height + 2 * HALF))
    for g in range(8):
        for k in range(0, 8, 2):
            parts = [jnp.concatenate([top[g, i], own[g, i], bottom[g, i]], axis=0) for i in (k, k + 1)]
            both = dot(weights, jnp.concatenate(parts, axis=1))
            upper, lower = split(both[:height] + both[height:])
            high[g, k], high[g, k + 1] = upper[:, :width], upper[:, width:]
            low[g, k], low[g, k + 1] = lower[:, :width], lower[:, width:]


def mixed(a, b):
    lane = lax.broadcasted_iota(jnp.int32, a.shape, 1)
    even = (lane // HALF) % 2 == 0
    a, b = a.astype(F32), b.astype(F32)
    return jnp.concatenate([jnp.where(even, a, b), jnp.where(even, b, a)], axis=1).astype(BF16)


def columns_kernel(high, low, left, right, across, flat, halo_high, halo_low):
    height, width = high.shape[2:]
    row, col = indices(height, height)
    weights = row_weights(row, col + HALF)
    for g in range(8):
        both = dot(weights, mixed(left[g], right[g]))
        upper, lower = split(both[:height] + both[height:])
        halo_high[g], halo_low[g] = upper, lower
    for k in range(8):
        lanes = slice(width * (k // 4), width * (k // 4 + 1))
        for g in range(8):
            upper = jnp.concatenate([high[g, k], halo_high[g, :, lanes]], axis=1)
            lower = jnp.concatenate([low[g, k], halo_low[g, :, lanes]], axis=1)
            both = dot(upper, across[k])
            value = both[:, :width] + both[:, width:] + dot(lower, across[k, :, :width])
            flat[pl.ds((8 * g + k) * (height + PAD), height), :] = value


def gram_kernel(points, height, flat, top, bottom, across, field, gram, edge):
    width, count, pitch, band_rows = flat.shape[1], 64, height + PAD, 2 * HALF + PAD
    row, col = indices(2 * HALF, 2 * HALF)
    row = jnp.where(row < HALF, row, row + height - 2 * HALF)
    col = jnp.where(col < HALF, col, col + height)
    weights = row_weights(row, col)
    uppers, lowers = [], []
    for g in range(8):
        a, b = [jnp.concatenate([top[i], bottom[i]], axis=0) for i in (g, 8 + g)]
        both = dot(weights, mixed(a, b))
        upper, lower = split(both[: 2 * HALF] + both[2 * HALF :])
        uppers.append(upper)
        lowers.append(lower)
    upper, lower = jnp.concatenate(uppers, axis=0), jnp.concatenate(lowers, axis=0)
    lane = lax.broadcasted_iota(jnp.int32, (2 * HALF, width), 1)
    inside = (lane < HALF) | (lane >= width - HALF)
    for h in range(2):
        lanes = slice(width * h, width * (h + 1))
        both = dot(upper[:, lanes], across[h])
        value = both[:, :width] + both[:, width:] + dot(lower[:, lanes], across[h, :, :width])
        for g in range(8):
            rows = value[2 * HALF * g : 2 * HALF * (g + 1)]
            for q in range(4):
                s = 8 * g + 4 * h + q
                added = jnp.where(inside, pltpu.roll(rows, width - HALF - 2 * HALF * q, 1), 0.0)
                edge[pl.ds(s * band_rows, HALF), :] = flat[pl.ds(s * pitch, HALF), :] + added[:HALF]
                edge[pl.ds(s * band_rows + HALF, HALF), :] = (
                    flat[pl.ds(s * pitch + height - HALF, HALF), :] + added[HALF:]
                )
    for r in range(height):
        if HALF <= r < height - HALF:
            value = flat[pl.ds(r, count, stride=pitch), :]
        else:
            start = r if r < HALF else r - height + 2 * HALF
            value = edge[pl.ds(start, count, stride=band_rows), :]
        upper, lower = split(value)
        field[:count, r * width : (r + 1) * width] = upper
        field[count:, r * width : (r + 1) * width] = lower
    total = jnp.zeros((2 * count, 2 * count), F32)
    size = 2048
    for start in range(0, height * width, size):
        part = field[:, start : start + size]
        total = total + lax.dot_general(part, part, (((1,), (1,)), ((), ())), preferred_element_type=F32)
    total = total[:count, :count] + total[count:, count:] + (total[:count, count:] + total[count:, :count])
    gram[...] = total / points


def factor(gram, size=8):
    count = gram.shape[0]
    row = lax.broadcasted_iota(jnp.int32, gram.shape, 0)
    col = lax.broadcasted_iota(jnp.int32, gram.shape, 1)
    a = jnp.concatenate([gram, jnp.where(row == col, 1.0, 0.0).astype(F32)], axis=1)
    rows = []
    for k in range(0, count, size):
        columns = [jnp.broadcast_to(a[:, k + i : k + i + 1], a.shape) for i in range(size)]
        lower, scale = {}, []
        for j in range(size):
            pivot = columns[j][k + j : k + j + 1]
            for m in range(j):
                pivot = pivot - lower[j, m] * lower[j, m]
            scale.append(lax.rsqrt(pivot))
            for i in range(j + 1, size):
                entry = columns[j][k + i : k + i + 1]
                for m in range(j):
                    entry = entry - lower[i, m] * lower[j, m]
                lower[i, j] = entry * scale[j]

        def solve(values):
            done = []
            for i in range(size):
                value = values[i]
                for m in range(i):
                    value = value - lower[i, m] * done[m]
                done.append(value * scale[i])
            return done

        new = solve([a[k + i : k + i + 1] for i in range(size)])
        rows += new
        if k + size < count:
            multipliers = solve(columns)
            for m in range(size):
                a = a - multipliers[m] * new[m]
    return rows


def basis_kernel(gram, field, basis, upper, work, inverse):
    count = gram.shape[0]

    @pl.when(pl.program_id(0) == 0)
    def _():
        for k, value in enumerate(factor(gram[...])):
            work[k : k + 1, :] = value
        row = lax.broadcasted_iota(jnp.int32, (count, count), 0)
        col = lax.broadcasted_iota(jnp.int32, (count, count), 1)
        both = work[...]
        upper[...] = jnp.where(row <= col, both[:, :count], 0.0)
        high, low = split(jnp.where(row >= col, both[:, count:], 0.0))
        top = jnp.concatenate([high, high], axis=1)
        bottom = jnp.concatenate([low, jnp.zeros_like(low)], axis=1)
        inverse[...] = jnp.concatenate([top, bottom], axis=0)

    width = basis.shape[2]
    both = dot(inverse[...], field[...])
    value = both[:count] + both[count:]
    for r in range(basis.shape[1]):
        basis[:, r, :] = value[:, r * width : (r + 1) * width]


def whole(n):
    return [pl.BlockSpec(memory_space=pltpu.VMEM)] * n


def shape(*dims, dtype=BF16):
    return jax.ShapeDtypeStruct(dims, dtype)


def edges(own):
    height, width = own.shape[2:]
    return pl.pallas_call(
        edges_kernel,
        out_shape=[shape(8, height, width)] * 2 + [shape(8, 8, HALF, width)] * 2,
        in_specs=whole(1),
        out_specs=whole(4),
        compiler_params=pltpu.CompilerParams(vmem_limit_bytes=16 << 20),
        cost_estimate=pl.CostEstimate(
            flops=4 * width * own.size, bytes_accessed=3 * own.size, transcendentals=0
        ),
    )(own)


def filter_rows(top, own, bottom):
    height, width = own.shape[2:]
    return pl.pallas_call(
        rows_kernel,
        out_shape=[shape(8, 8, height, width)] * 2,
        in_specs=whole(3),
        out_specs=whole(2),
        compiler_params=pltpu.CompilerParams(vmem_limit_bytes=16 << 20),
        cost_estimate=pl.CostEstimate(
            flops=4 * own.size * (height + 2 * HALF), bytes_accessed=6 * own.size, transcendentals=0
        ),
    )(top, own, bottom)


def filter_columns(high, low, left, right):
    height, width = high.shape[2:]
    return pl.pallas_call(
        columns_kernel,
        out_shape=shape(64 * (height + PAD), width, dtype=F32),
        in_specs=whole(5),
        out_specs=whole(1)[0],
        compiler_params=pltpu.CompilerParams(vmem_limit_bytes=16 << 20),
        scratch_shapes=[pltpu.VMEM((8, height, 2 * width), BF16)] * 2,
        cost_estimate=pl.CostEstimate(
            flops=12 * width * high.size, bytes_accessed=8 * high.size, transcendentals=0
        ),
    )(high, low, left, right, jnp.asarray(column_weights(width)))


def correlate(flat, top, bottom, height, points):
    width = flat.shape[1]
    return pl.pallas_call(
        functools.partial(gram_kernel, points, height),
        out_shape=[shape(128, height * width), shape(64, 64, dtype=F32)],
        in_specs=whole(4),
        out_specs=whole(2),
        compiler_params=pltpu.CompilerParams(vmem_limit_bytes=16 << 20),
        scratch_shapes=[pltpu.VMEM((64 * (2 * HALF + PAD), width), F32)],
    )(flat, top, bottom, jnp.asarray(edge_column_weights(width)))


def orthonormal(gram, field, height, width):
    count = gram.shape[0]
    return pl.pallas_call(
        basis_kernel,
        grid=(height // STEP,),
        compiler_params=pltpu.CompilerParams(vmem_limit_bytes=24 << 20),
        out_shape=[shape(count, height, width, dtype=F32), shape(count, count, dtype=F32)],
        in_specs=[pl.BlockSpec((count, count), lambda i: (0, 0)), pl.BlockSpec((2 * count, STEP * width), lambda i: (0, i))],
        out_specs=[pl.BlockSpec((count, STEP, width), lambda i: (0, i, 0)), pl.BlockSpec((count, count), lambda i: (0, 0))],
        scratch_shapes=[pltpu.VMEM((count, 2 * count), F32), pltpu.VMEM((2 * count, 2 * count), BF16)],
    )(gram, field)


def pack(gram):
    half = gram.shape[0] // 2
    first, second = gram[:half, :half], gram[half:, half:]
    row = lax.broadcasted_iota(jnp.int32, (half, half), 0)
    col = lax.broadcasted_iota(jnp.int32, (half, half), 1)
    mixed = jnp.where(row >= col, first, second)
    diagonal = jnp.sum(jnp.where(row == col, second, 0.0), axis=0)
    diagonal = jnp.pad(diagonal, (0, half))[None]
    top = jnp.concatenate([gram[half:, :half], mixed], axis=1)
    return jnp.concatenate([top, diagonal, jnp.zeros_like(diagonal)], axis=0)


def unpack(packed):
    half = packed.shape[1] // 2
    cross, mixed, diagonal = packed[:half, :half], packed[:half, half:], packed[half, :half]
    row = lax.broadcasted_iota(jnp.int32, (half, half), 0)
    col = lax.broadcasted_iota(jnp.int32, (half, half), 1)
    first = jnp.where(row >= col, mixed, mixed.T)
    second = jnp.where(row < col, mixed, mixed.T)
    second = jnp.where(row == col, diagonal[None], second)
    return jnp.concatenate(
        [jnp.concatenate([first, cross.T], axis=1), jnp.concatenate([cross, second], axis=1)], axis=0
    )


def summed(array, axis):
    copies = jnp.broadcast_to(array[None], (lax.axis_size(axis),) + array.shape)
    return lax.all_to_all(copies, axis, 0, 0).sum(0)


def swap(upward, downward, axis):
    devices = lax.axis_size(axis)
    up = [(i, (i + 1) % devices) for i in range(devices)]
    down = [(j, i) for i, j in up]
    first = lax.ppermute(upward, axis, up)
    second = lax.ppermute(downward, axis, down)
    return first, second


def program(snapshots):
    count, height, width = snapshots.shape
    points = height * width * lax.axis_size("row") * lax.axis_size("col")
    own = snapshots.reshape(8, 8, height, width)
    last_columns, first_columns, last_rows, first_rows = edges(own)
    sides = swap(last_columns, first_columns, "col")
    top, bottom = swap(last_rows, first_rows, "row")
    last_rows, first_rows = [
        jnp.concatenate([side[:, rows] for side in sides], axis=0) for rows in (slice(height - HALF, None), slice(HALF))
    ]
    corners = swap(last_rows, first_rows, "row")
    high, low = filter_rows(top, own, bottom)
    flat = filter_columns(high, low, *sides)
    field, gram = correlate(flat, *corners, height, points)
    total = pack(gram).reshape(-1)
    total = summed(summed(total, "row"), "col")
    gram = unpack(total.reshape(count // 2 + 2, count))
    return tuple(orthonormal(gram, field, height, width))


def solution(mesh):
    return jax.shard_map(
        program,
        mesh=mesh,
        in_specs=(P(None, "row", "col"),),
        out_specs=(P(None, "row", "col"), P()),
        check_vma=False,
    )
```

```python
import functools
import jax
import jax.numpy as jnp
import numpy as np
from jax import lax
from jax.experimental import pallas as pl
from jax.experimental.pallas import tpu as pltpu
from jax.sharding import PartitionSpec as P


HALF = 16
TAPS = 2 * HALF + 1
BF16, F32 = jnp.bfloat16, jnp.float32
STEP = 48
PAD = 8


def band(length):
    sigma = HALF / 3.0
    offsets = np.arange(TAPS) - HALF
    weights = np.exp(-offsets * offsets / (2.0 * sigma * sigma))
    weights = weights / weights.sum()
    result = np.zeros((length + 2 * HALF, length), np.float64)
    for inner in range(length):
        result[inner : inner + TAPS, inner] = weights
    return result


def two(matrix):
    high = np.asarray(matrix, np.float32).astype(BF16)
    low = (matrix - high.astype(np.float64)).astype(np.float32).astype(BF16)
    return high, low


def row_weights(row, col):
    sigma = HALF / 3.0
    offsets = np.arange(TAPS) - HALF
    total = float(np.exp(-offsets * offsets / (2.0 * sigma * sigma)).sum())
    spread = col - row
    shifted = (spread - HALF).astype(F32)
    value = jnp.exp(shifted * shifted * (-0.5 / (sigma * sigma))) * (1.0 / total)
    value = jnp.where((spread >= 0) & (spread <= 2 * HALF), value, 0.0)
    return jnp.concatenate(split(value), axis=0)


def indices(rows, cols):
    return [lax.broadcasted_iota(jnp.int32, (rows, cols), i) for i in range(2)]


def edge_column_weights(width):
    matrix = band(width)
    edge = np.r_[width - HALF : width, :HALF]
    left, right = matrix[:HALF, edge], matrix[HALF + width :, edge]
    result = []
    for pair in ((left, right), (right, left)):
        block = np.concatenate(pair, axis=0)
        result.append(np.concatenate(two(np.kron(np.eye(4), block)), axis=1))
    return np.stack(result)


def column_weights(width):
    matrix = band(width)
    left, own, right = matrix[:HALF], matrix[HALF : HALF + width], matrix[HALF + width :]
    result = []
    for h in range(2):
        for q in range(4):
            halo = np.zeros((width, width))
            first, second = (left, right) if h == 0 else (right, left)
            halo[32 * q : 32 * q + HALF] = first
            halo[32 * q + HALF : 32 * q + 2 * HALF] = second
            result.append(np.concatenate(two(np.concatenate([own, halo], axis=0)), axis=1))
    return np.stack(result)


def dot(a, b):
    return jnp.dot(a, b, preferred_element_type=F32)


def split(value):
    high = value.astype(BF16)
    return high, (value - high.astype(F32)).astype(BF16)


def selector(width):
    row = lax.broadcasted_iota(jnp.int32, (width, width), 0)
    shift = lax.broadcasted_iota(jnp.int32, (width, width), 1) - row
    blocks = []
    for k in range(8):
        h, q = k // 4, k % 4
        last = (shift == 32 * q + HALF * h + HALF - width) & (row >= width - HALF)
        first = (shift == 32 * q + HALF * (1 - h)) & (row < HALF)
        both = [jnp.where(mask, 1.0, 0.0).astype(BF16) for mask in (last, first)]
        blocks.append(jnp.concatenate(both, axis=1))
    return jnp.concatenate(blocks, axis=0)


def edges_kernel(own, last_columns, first_columns, last_rows, first_rows):
    height, width = own.shape[2:]
    parts = [jnp.concatenate([own[g, k] for k in range(8)], axis=1) for g in range(8)]
    both = dot(jnp.concatenate(parts, axis=0), selector(width)).astype(BF16)
    for g in range(8):
        last_columns[g] = both[g * height : (g + 1) * height, :width]
        first_columns[g] = both[g * height : (g + 1) * height, width:]
    last_rows[...] = own[:, :, height - HALF :, :]
    first_rows[...] = own[:, :, :HALF, :]


def rows_kernel(top, own, bottom, high, low):
    height, width = own.shape[2:]
    weights = row_weights(*indices(height, height + 2 * HALF))
    for g in range(8):
        for k in range(0, 8, 2):
            parts = [jnp.concatenate([top[g, i], own[g, i], bottom[g, i]], axis=0) for i in (k, k + 1)]
            both = dot(weights, jnp.concatenate(parts, axis=1))
            upper, lower = split(both[:height] + both[height:])
            high[g, k], high[g, k + 1] = upper[:, :width], upper[:, width:]
            low[g, k], low[g, k + 1] = lower[:, :width], lower[:, width:]


def mixed(a, b):
    lane = lax.broadcasted_iota(jnp.int32, a.shape, 1)
    even = (lane // HALF) % 2 == 0
    a, b = a.astype(F32), b.astype(F32)
    return jnp.concatenate([jnp.where(even, a, b), jnp.where(even, b, a)], axis=1).astype(BF16)


def columns_kernel(high, low, left, right, across, flat, halo_high, halo_low):
    height, width = high.shape[2:]
    row, col = indices(height, height)
    weights = row_weights(row, col + HALF)
    for g in range(8):
        both = dot(weights, mixed(left[g], right[g]))
        upper, lower = split(both[:height] + both[height:])
        halo_high[g], halo_low[g] = upper, lower
    for k in range(8):
        lanes = slice(width * (k // 4), width * (k // 4 + 1))
        for g in range(8):
            upper = jnp.concatenate([high[g, k], halo_high[g, :, lanes]], axis=1)
            lower = jnp.concatenate([low[g, k], halo_low[g, :, lanes]], axis=1)
            both = dot(upper, across[k])
            value = both[:, :width] + both[:, width:] + dot(lower, across[k, :, :width])
            flat[pl.ds((8 * g + k) * (height + PAD), height), :] = value


def gram_kernel(points, height, flat, top, bottom, across, field, gram, edge):
    width, count, pitch, band_rows = flat.shape[1], 64, height + PAD, 2 * HALF + PAD
    row, col = indices(2 * HALF, 2 * HALF)
    row = jnp.where(row < HALF, row, row + height - 2 * HALF)
    col = jnp.where(col < HALF, col, col + height)
    weights = row_weights(row, col)
    uppers, lowers = [], []
    for g in range(8):
        a, b = [jnp.concatenate([top[i], bottom[i]], axis=0) for i in (g, 8 + g)]
        both = dot(weights, mixed(a, b))
        upper, lower = split(both[: 2 * HALF] + both[2 * HALF :])
        uppers.append(upper)
        lowers.append(lower)
    upper, lower = jnp.concatenate(uppers, axis=0), jnp.concatenate(lowers, axis=0)
    lane = lax.broadcasted_iota(jnp.int32, (2 * HALF, width), 1)
    inside = (lane < HALF) | (lane >= width - HALF)
    for h in range(2):
        lanes = slice(width * h, width * (h + 1))
        both = dot(upper[:, lanes], across[h])
        value = both[:, :width] + both[:, width:] + dot(lower[:, lanes], across[h, :, :width])
        for g in range(8):
            rows = value[2 * HALF * g : 2 * HALF * (g + 1)]
            for q in range(4):
                s = 8 * g + 4 * h + q
                added = jnp.where(inside, pltpu.roll(rows, width - HALF - 2 * HALF * q, 1), 0.0)
                edge[pl.ds(s * band_rows, HALF), :] = flat[pl.ds(s * pitch, HALF), :] + added[:HALF]
                edge[pl.ds(s * band_rows + HALF, HALF), :] = (
                    flat[pl.ds(s * pitch + height - HALF, HALF), :] + added[HALF:]
                )
    for r in range(height):
        if HALF <= r < height - HALF:
            value = flat[pl.ds(r, count, stride=pitch), :]
        else:
            start = r if r < HALF else r - height + 2 * HALF
            value = edge[pl.ds(start, count, stride=band_rows), :]
        upper, lower = split(value)
        field[:count, r * width : (r + 1) * width] = upper
        field[count:, r * width : (r + 1) * width] = lower
    total = jnp.zeros((2 * count, 2 * count), F32)
    size = 2048
    for start in range(0, height * width, size):
        part = field[:, start : start + size]
        total = total + lax.dot_general(part, part, (((1,), (1,)), ((), ())), preferred_element_type=F32)
    total = total[:count, :count] + total[count:, count:] + (total[:count, count:] + total[count:, :count])
    total = total / points
    half = count // 2
    row, col = indices(half, half)
    second = total[half:, half:]
    diagonal = jnp.sum(jnp.where(row == col, second, 0.0), axis=0, keepdims=True)
    gram[:half, :] = jnp.concatenate([jnp.where(row <= col, total[:half, :half], second), total[:half, half:]], axis=1)
    gram[half : half + 1, :] = jnp.concatenate([diagonal, jnp.zeros_like(diagonal)], axis=1)
    gram[half + 1 :, :] = jnp.zeros((1, count), F32)


def factor(gram, size=8):
    count = gram.shape[0]
    row = lax.broadcasted_iota(jnp.int32, gram.shape, 0)
    col = lax.broadcasted_iota(jnp.int32, gram.shape, 1)
    a = jnp.concatenate([gram, jnp.where(row == col, 1.0, 0.0).astype(F32)], axis=1)
    rows = []
    for k in range(0, count, size):
        columns = [jnp.broadcast_to(a[:, k + i : k + i + 1], a.shape) for i in range(size)]
        lower, scale = {}, []
        for j in range(size):
            pivot = columns[j][k + j : k + j + 1]
            for m in range(j):
                pivot = pivot - lower[j, m] * lower[j, m]
            scale.append(lax.rsqrt(pivot))
            for i in range(j + 1, size):
                entry = columns[j][k + i : k + i + 1]
                for m in range(j):
                    entry = entry - lower[i, m] * lower[j, m]
                lower[i, j] = entry * scale[j]

        def solve(values):
            done = []
            for i in range(size):
                value = values[i]
                for m in range(i):
                    value = value - lower[i, m] * done[m]
                done.append(value * scale[i])
            return done

        new = solve([a[k + i : k + i + 1] for i in range(size)])
        rows += new
        if k + size < count:
            multipliers = solve(columns)
            for m in range(size):
                a = a - multipliers[m] * new[m]
    return rows


def unpack(packed):
    half = packed.shape[1] // 2
    mixture, cross, diagonal = packed[:half, :half], packed[:half, half:], packed[half : half + 1, :half]
    row, col = indices(half, half)
    other = mixture.T
    first = jnp.where(row <= col, mixture, other)
    second = jnp.where(row > col, mixture, other)
    second = jnp.where(row == col, diagonal, second)
    top = jnp.concatenate([first, cross], axis=1)
    return jnp.concatenate([top, jnp.concatenate([cross.T, second], axis=1)], axis=0)


def basis_kernel(gram, field, basis, upper, work, inverse):
    count = gram.shape[1]

    @pl.when(pl.program_id(0) == 0)
    def _():
        for k, value in enumerate(factor(unpack(gram[...]))):
            work[k : k + 1, :] = value
        row = lax.broadcasted_iota(jnp.int32, (count, count), 0)
        col = lax.broadcasted_iota(jnp.int32, (count, count), 1)
        both = work[...]
        upper[...] = jnp.where(row <= col, both[:, :count], 0.0)
        high, low = split(jnp.where(row >= col, both[:, count:], 0.0))
        top = jnp.concatenate([high, high], axis=1)
        bottom = jnp.concatenate([low, jnp.zeros_like(low)], axis=1)
        inverse[...] = jnp.concatenate([top, bottom], axis=0)

    width = basis.shape[2]
    both = dot(inverse[...], field[...])
    value = both[:count] + both[count:]
    for r in range(basis.shape[1]):
        basis[:, r, :] = value[:, r * width : (r + 1) * width]


def whole(n):
    return [pl.BlockSpec(memory_space=pltpu.VMEM)] * n


def shape(*dims, dtype=BF16):
    return jax.ShapeDtypeStruct(dims, dtype)


def edges(own):
    height, width = own.shape[2:]
    return pl.pallas_call(
        edges_kernel,
        out_shape=[shape(8, height, width)] * 2 + [shape(8, 8, HALF, width)] * 2,
        in_specs=whole(1),
        out_specs=whole(4),
        compiler_params=pltpu.CompilerParams(vmem_limit_bytes=16 << 20),
        cost_estimate=pl.CostEstimate(
            flops=4 * width * own.size, bytes_accessed=3 * own.size, transcendentals=0
        ),
    )(own)


def filter_rows(top, own, bottom):
    height, width = own.shape[2:]
    return pl.pallas_call(
        rows_kernel,
        out_shape=[shape(8, 8, height, width)] * 2,
        in_specs=whole(3),
        out_specs=whole(2),
        compiler_params=pltpu.CompilerParams(vmem_limit_bytes=16 << 20),
        cost_estimate=pl.CostEstimate(
            flops=4 * own.size * (height + 2 * HALF), bytes_accessed=6 * own.size, transcendentals=0
        ),
    )(top, own, bottom)


def filter_columns(high, low, left, right):
    height, width = high.shape[2:]
    return pl.pallas_call(
        columns_kernel,
        out_shape=shape(64 * (height + PAD), width, dtype=F32),
        in_specs=whole(5),
        out_specs=whole(1)[0],
        compiler_params=pltpu.CompilerParams(vmem_limit_bytes=16 << 20),
        scratch_shapes=[pltpu.VMEM((8, height, 2 * width), BF16)] * 2,
        cost_estimate=pl.CostEstimate(
            flops=12 * width * high.size, bytes_accessed=8 * high.size, transcendentals=0
        ),
    )(high, low, left, right, jnp.asarray(column_weights(width)))


def correlate(flat, top, bottom, height, points):
    width = flat.shape[1]
    return pl.pallas_call(
        functools.partial(gram_kernel, points, height),
        out_shape=[shape(128, height * width), shape(34, 64, dtype=F32)],
        in_specs=whole(4),
        out_specs=whole(2),
        compiler_params=pltpu.CompilerParams(vmem_limit_bytes=16 << 20),
        scratch_shapes=[pltpu.VMEM((64 * (2 * HALF + PAD), width), F32)],
    )(flat, top, bottom, jnp.asarray(edge_column_weights(width)))


def orthonormal(gram, field, height, width):
    count = gram.shape[1]
    return pl.pallas_call(
        basis_kernel,
        grid=(height // STEP,),
        compiler_params=pltpu.CompilerParams(vmem_limit_bytes=24 << 20),
        out_shape=[shape(count, height, width, dtype=F32), shape(count, count, dtype=F32)],
        in_specs=[pl.BlockSpec(gram.shape, lambda i: (0, 0)), pl.BlockSpec((2 * count, STEP * width), lambda i: (0, i))],
        out_specs=[pl.BlockSpec((count, STEP, width), lambda i: (0, i, 0)), pl.BlockSpec((count, count), lambda i: (0, 0))],
        scratch_shapes=[pltpu.VMEM((count, 2 * count), F32), pltpu.VMEM((2 * count, 2 * count), BF16)],
    )(gram, field)


def summed(array, axis):
    copies = jnp.broadcast_to(array[None], (lax.axis_size(axis),) + array.shape)
    return lax.all_to_all(copies, axis, 0, 0).sum(0)


def swap(upward, downward, axis):
    devices = lax.axis_size(axis)
    up = [(i, (i + 1) % devices) for i in range(devices)]
    down = [(j, i) for i, j in up]
    first = lax.ppermute(upward, axis, up)
    second = lax.ppermute(downward, axis, down)
    return first, second


def program(snapshots):
    count, height, width = snapshots.shape
    points = height * width * lax.axis_size("row") * lax.axis_size("col")
    own = snapshots.reshape(8, 8, height, width)
    last_columns, first_columns, last_rows, first_rows = edges(own)
    sides = swap(last_columns, first_columns, "col")
    top, bottom = swap(last_rows, first_rows, "row")
    last_rows, first_rows = [
        jnp.concatenate([side[:, rows] for side in sides], axis=0) for rows in (slice(height - HALF, None), slice(HALF))
    ]
    corners = swap(last_rows, first_rows, "row")
    high, low = filter_rows(top, own, bottom)
    flat = filter_columns(high, low, *sides)
    field, gram = correlate(flat, *corners, height, points)
    total = summed(summed(gram.reshape(-1), "row"), "col")
    gram = total.reshape(count // 2 + 2, count)
    return tuple(orthonormal(gram, field, height, width))


def solution(mesh):
    return jax.shard_map(
        program,
        mesh=mesh,
        in_specs=(P(None, "row", "col"),),
        out_specs=(P(None, "row", "col"), P()),
        check_vma=False,
    )
```
